32 devices in a mesh: rows: 8 (over y, x, core), depth: 4 (over z).
Axes of the slice: x: 2, y: 2, z: 4, core: 2. Of those that a mesh axis runs over, the one named last changes fastest.
Arguments:
- left_factors: bfloat16 [8, 8, 2048, 128], P('rows', 'depth'), may hold values from -0.125 to 0.125
- right_factors: bfloat16 [8, 8, 2048, 128], P('rows', 'depth'), may hold values from -0.125 to 0.125
- probe_matrix: bfloat16 [2048, 128], replicated, may hold values from -6 to 6
- tile_list: int32 [8, 4], replicated, may hold values from 0 to 7, all different within a row
Outputs:
- basis: float32 [8, 4, 2048, 128], P('rows', None, 'depth')
- chol_factor: float32 [8, 4, 128, 128], P('rows')
The draws below stay inside these ranges and needn't reach their ends.
Inputs may be any that keep to these rules, and one draw needn't show every extreme that they name: `tile_list`: each row holds 4 different tile rows, and every tile row is named by some row.
All inputs are finite; a program needn't handle non-finite values.
Results may differ from the reference program's by a relative error of at most 0.0058.
Values may be sent and summed in bfloat16 or wider, within the bound.
No kernel may reach another device: no remote copies, remote signals or barrier semaphores. Data moves between devices by JAX's collectives and lax.ppermute only.
A program may use at most 64 MiB of HBM per device.

```python
import math
import jax
import jax.numpy as jnp
from jax import lax

TILE = 2048
RANK = 128
TLIST = 4
NTILE = 8
PANELS = 8


def shard_levels(own_key, dims, split, smallest, largest):
    gain, own = 1.0, jax.random.fold_in(own_key, 6)
    for axis_at, parts in split:
        heights = jnp.exp(jax.random.uniform(jax.random.fold_in(own, axis_at), (parts,), jnp.float32, smallest / len(split), largest / len(split)))
        gain = gain * jnp.repeat(heights, dims[axis_at] // parts).reshape([-1 if axis == axis_at else 1 for axis in range(len(dims))])
    return gain


def distinct(own_key, rows, number_of, top, lift):
    ranking = jax.random.permutation(jax.random.fold_in(own_key, 1), number_of)
    favour = ranking
    for power in range(3):
        favour = favour * favour // number_of
    favour = favour * lift // number_of
    lots = jax.random.randint(jax.random.fold_in(own_key, 2), (rows, number_of), 0, 4096) + favour
    holders = jax.random.permutation(jax.random.fold_in(own_key, 3), rows)[jnp.arange(number_of) % rows]
    lots = jnp.where(jnp.arange(rows)[:, None] == holders[None, :], 1 << 14, lots)
    merit = lots * number_of + jnp.arange(number_of)
    return lax.top_k(merit.astype(jnp.int32), top)[1].astype(jnp.int32)


def scatter_about(stream_key, extent, deviation, bound, split=(), kind=jnp.bfloat16):
    result = jax.random.normal(stream_key, extent, jnp.float32) * deviation
    if len(split) > 0:
        result = shard_levels(stream_key, extent, split, -0.22, 0.18) * result
    return jnp.clip(result, min=-bound, max=bound).astype(kind)


def setup_inputs(seed: int = 0) -> dict:
    keys = jax.random.split(jax.random.key(seed), 5)
    return {
        "left_factors": scatter_about(keys[0], (NTILE, PANELS, TILE, RANK), TILE ** -0.5, 0.125, ((0, 8), (1, 4))),
        "right_factors": scatter_about(keys[1], (NTILE, PANELS, TILE, RANK), TILE ** -0.5, 0.125, ((0, 8), (1, 4))),
        "probe_matrix": scatter_about(keys[2], (TILE, RANK), 1.0, 6.0),
        "tile_list": distinct(keys[3], NTILE, NTILE, TLIST, 8192),
    }


def reference(left_factors, right_factors, probe_matrix, tile_list):
    probe32 = probe_matrix.astype(jnp.float32)

    def sketch_one(pair):
        left_row, right_row = pair
        image = jnp.einsum('pbk,bl->pkl', left_row.astype(jnp.float32), probe32).astype(jnp.bfloat16)
        return jnp.einsum('pbk,pkl->pbl', right_row.astype(jnp.float32), image.astype(jnp.float32)).astype(jnp.bfloat16)
    sketch_rows = lax.map(sketch_one, (left_factors, right_factors))
    scale = math.sqrt(float(TILE))

    def update_row(triple):
        left_row, right_row, listed = triple
        picked = jnp.take(sketch_rows, listed.astype(jnp.int32), axis=0)
        coupling = jnp.einsum('pbk,tpbl->tpkl', right_row.astype(jnp.float32), picked.astype(jnp.float32)).astype(jnp.bfloat16)
        sketch = jnp.einsum('pbk,tpkl->tbl', left_row.astype(jnp.float32), coupling.astype(jnp.float32))
        gram = jnp.einsum('tbk,tbl->tkl', sketch, sketch, precision=lax.Precision.HIGHEST)
        lower = jnp.linalg.cholesky(gram)
        solved = jax.scipy.linalg.solve_triangular(lower, jnp.transpose(sketch, (0, 2, 1)), lower=True)
        return (jnp.transpose(solved, (0, 2, 1)) * scale, lower / scale)
    basis, chol_factor = lax.map(update_row, (left_factors, right_factors, tile_list))
    return (basis, chol_factor)
```

```python
import functools
import math

import jax
import jax.numpy as jnp
from jax import lax
from jax.experimental import pallas as pl
from jax.experimental.pallas import tpu as pltpu
from jax.sharding import PartitionSpec as P


HIGHEST = lax.Precision.HIGHEST
BLOCK = 8


def swap(x, axis, bits, size):
    return lax.ppermute(x, axis, [(i, i ^ bits) for i in range(size)])


def gather_rows(block, axis, size):
    known = {0: block}
    if size & (size - 1):
        every = lax.all_gather(block, axis)
        me = lax.axis_index(axis)
        return {
            o: lax.dynamic_index_in_dim(every, (me + o) % size, 0, keepdims=False)
            for o in range(size)
        }
    bits = [1 << b for b in range(size.bit_length() - 1)]
    single = bits[:1] if len(bits) % 2 else []
    pairs = bits[len(single):]
    for a, b in zip(pairs[::2], pairs[1::2]):
        fresh = {}
        for o, have in known.items():
            half = have.shape[0] // 2
            from_a = swap(have, axis, a, size)
            from_b = swap(have, axis, b, size)
            low = swap(from_b[:half], axis, a, size)
            high = swap(from_a[half:], axis, b, size)
            fresh[o ^ a] = from_a
            fresh[o ^ b] = from_b
            fresh[o ^ a ^ b] = (low, high)
        known.update(fresh)
        known = {
            o: jnp.concatenate(v, axis=0) if isinstance(v, tuple) and size > 8 else v
            for o, v in known.items()
        }
    for a in single:
        known.update(
            {o ^ a: jax.tree.map(lambda v: swap(v, axis, a, size), have) for o, have in known.items()}
        )
    return known


def coupling_of(right, found):
    dims = (((0,), (0,)), ((), ()))
    if not isinstance(found, tuple):
        return lax.dot_general(right, found, dims, preferred_element_type=jnp.float32)
    half = found[0].shape[0]
    return lax.dot_general(
        right[:half], found[0], dims, preferred_element_type=jnp.float32
    ) + lax.dot_general(right[half:], found[1], dims, preferred_element_type=jnp.float32)


def sketch_kernel(count, panels, *refs):
    left_refs, coupling_refs = refs[:count], refs[count:count + count * panels]
    sketch_ref, gram_ref = refs[count + count * panels:]
    for t in range(sketch_ref.shape[0]):
        total = None
        for o in range(count):
            for p in range(panels):
                term = jnp.dot(
                    left_refs[o][p],
                    coupling_refs[o * panels + p][t],
                    preferred_element_type=jnp.float32,
                )
                total = term if total is None else total + term
        sketch_ref[t] = total
        gram_ref[t] = lax.dot_general(
            total, total, (((0,), (0,)), ((), ())), precision=HIGHEST,
            preferred_element_type=jnp.float32,
        )


def eliminate(panel, first, lane, sub):
    cols = [
        jnp.broadcast_to(panel[:, first + j:first + j + 1], panel.shape) for j in range(BLOCK)
    ]
    upper = jnp.zeros_like(panel)
    inverse = jnp.zeros_like(panel)
    pivots = jnp.zeros_like(panel)
    for j in range(BLOCK):
        k = first + j
        pivot = jnp.broadcast_to(cols[j][j:j + 1, :], panel.shape)
        recip = 1.0 / pivot
        root = lax.rsqrt(pivot)
        factor = jnp.where(sub > j, cols[j] * recip, 0.0)
        for c in range(j + 1, BLOCK):
            cols[c] = cols[c] - factor * jnp.broadcast_to(cols[c][j:j + 1, :], panel.shape)
        row = jnp.broadcast_to(panel[j:j + 1, :], panel.shape)
        here = sub == j
        upper = jnp.where(here & (lane >= k), row * root, upper)
        row = jnp.where(lane == k, 1.0, row)
        inverse = jnp.where(here & (lane <= k), row * root, inverse)
        pivots = jnp.where(here, recip, pivots)
        panel = jnp.where((lane == k) & (sub >= j), jnp.where(here, 1.0, 0.0), panel)
        panel = panel - factor * row
    below = jnp.where(lane >= first + BLOCK, panel * pivots, 0.0)
    panel = jnp.where((lane < first + BLOCK) & (lane > first + sub), 0.0, panel)
    return panel, below, upper, inverse


def factor_kernel(count, scale, *refs):
    gram_refs, sketch_ref = refs[:count], refs[count]
    basis_ref, chol_ref, work_ref, upper_ref, inverse_ref = refs[count + 1:]
    listed, width, _ = work_ref.shape
    terms = [ref[...] for ref in gram_refs]
    while len(terms) > 1:
        terms = [a + b for a, b in zip(terms[::2], terms[1::2])]
    work_ref[...] = terms[0]
    lane = lax.broadcasted_iota(jnp.int32, (BLOCK, width), 1)
    sub = lax.broadcasted_iota(jnp.int32, (BLOCK, width), 0)
    for first in range(0, width, BLOCK):
        last = first + BLOCK
        done = [eliminate(work_ref[t, first:last, :], first, lane, sub) for t in range(listed)]
        for t in range(listed):
            rows, below, upper, inverse = done[t]
            upper_ref[t, first:last, :] = upper
            inverse_ref[t, first:last, :] = inverse * scale
            if last < width:
                at = lax.broadcasted_iota(jnp.int32, (width - last, width), 1)
                old = work_ref[t, last:, :]
                old = jnp.where((at >= first) & (at < last), 0.0, old)
                update = lax.dot_general(
                    below, rows, (((0,), (0,)), ((), ())), precision=HIGHEST,
                    preferred_element_type=jnp.float32,
                )
                work_ref[t, last:, :] = old - update[last:, :]
    for t in range(listed):
        chol_ref[t] = upper_ref[t].T * (1.0 / scale)
        basis_ref[t] = lax.dot_general(
            sketch_ref[t], inverse_ref[t], (((1,), (1,)), ((), ())), precision=HIGHEST,
            preferred_element_type=jnp.float32,
        )


def on_device(rows_size, depth_size, left_factors, right_factors, probe_matrix, tile_list):
    left_own = left_factors[0]
    right_own = right_factors[0]
    panels, tile_size, rank_size = left_own.shape
    listed = tile_list.shape[1]
    width = probe_matrix.shape[1]
    scale = math.sqrt(float(tile_size))
    me = lax.axis_index("rows")
    level = lax.axis_index("depth")
    part = tile_size // depth_size

    image = jnp.einsum(
        "pbk,bl->pkl", left_own, probe_matrix, preferred_element_type=jnp.float32
    ).astype(jnp.bfloat16)
    sketch_rows = jnp.einsum(
        "pbk,pkl->pbl", right_own, image, preferred_element_type=jnp.float32
    ).astype(jnp.bfloat16)

    blocks = left_own.reshape(panels, depth_size, part, rank_size)
    power = depth_size & (depth_size - 1) == 0
    partner = [(level ^ o) if power else (level + o) % depth_size for o in range(depth_size)]

    def over_depth(x, o):
        if o == 0:
            return x
        if power:
            return swap(x, "depth", o, depth_size)
        return lax.ppermute(x, "depth", [((i + o) % depth_size, i) for i in range(depth_size)])

    def block_for(o):
        to = partner[o] if power else (level - o) % depth_size
        return lax.dynamic_index_in_dim(blocks, to, 1, keepdims=False)

    lefts = [over_depth(block_for(o), o) for o in range(depth_size)]

    mine = lax.dynamic_index_in_dim(tile_list, me, 0, keepdims=False)
    wanted = (mine ^ me) if rows_size & (rows_size - 1) == 0 else (mine - me) % rows_size
    couplings = []
    for p in range(panels):
        found = gather_rows(sketch_rows[p], "rows", rows_size)
        every = jnp.stack(
            [coupling_of(right_own[p], found[o]).astype(jnp.bfloat16) for o in range(rows_size)]
        )
        couplings.append(jnp.take(every, wanted, axis=0))
    gathered = [
        over_depth(couplings[p], o) for o in range(depth_size) for p in range(panels)
    ]

    vmem = pl.BlockSpec(memory_space=pltpu.VMEM)
    sketch, gram = pl.pallas_call(
        functools.partial(sketch_kernel, depth_size, panels),
        out_shape=(
            jax.ShapeDtypeStruct((listed, part, width), jnp.float32),
            jax.ShapeDtypeStruct((listed, width, width), jnp.float32),
        ),
        in_specs=[vmem] * (depth_size * (1 + panels)),
        out_specs=(vmem, vmem),
    )(*lefts, *gathered)
    grams = (
        [over_depth(gram, o) for o in range(depth_size)] if power else [lax.psum(gram, "depth")]
    )
    basis, chol_factor = pl.pallas_call(
        functools.partial(factor_kernel, len(grams), scale),
        out_shape=(
            jax.ShapeDtypeStruct((listed, part, width), jnp.float32),
            jax.ShapeDtypeStruct((listed, width, width), jnp.float32),
        ),
        in_specs=[vmem] * (len(grams) + 1),
        out_specs=(vmem, vmem),
        scratch_shapes=[pltpu.VMEM((listed, width, width), jnp.float32)] * 3,
    )(*grams, sketch)
    return (basis[None], chol_factor[None])


def solution(mesh):
    in_specs = (P("rows", "depth", None, None), P("rows", "depth", None, None), P(), P())
    out_specs = (P("rows", None, "depth", None), P("rows", None, None, None))
    body = functools.partial(on_device, mesh.shape["rows"], mesh.shape["depth"])
    return jax.shard_map(body, mesh=mesh, in_specs=in_specs, out_specs=out_specs, check_vma=False)
```

```python
import functools
import math

import jax
import jax.numpy as jnp
from jax import lax
from jax.experimental import pallas as pl
from jax.experimental.pallas import tpu as pltpu
from jax.sharding import PartitionSpec as P


HIGHEST = lax.Precision.HIGHEST
BLOCK = 8
VMEM = pl.BlockSpec(memory_space=pltpu.VMEM)
SMEM = pl.BlockSpec(memory_space=pltpu.SMEM)


def swap(x, axis, bits, size):
    return lax.ppermute(x, axis, [(i, i ^ bits) for i in range(size)])


def bits_of(size):
    return [1 << b for b in range(size.bit_length() - 1)]


def gather_rows(halves, axis, size):
    known = {0: halves}
    bits = bits_of(size)
    single = bits[:1] if len(bits) % 2 else []
    pairs = bits[len(single):]
    late = 0
    for a, b in zip(pairs[::2], pairs[1::2]):
        fresh = {}
        for o, (low, high) in known.items():
            a_low, b_low = swap(low, axis, a, size), swap(low, axis, b, size)
            b_high, a_high = swap(high, axis, b, size), swap(high, axis, a, size)
            fresh[o ^ a] = (a_low, a_high)
            fresh[o ^ b] = (b_low, b_high)
            fresh[o ^ a ^ b] = (swap(b_low, axis, a, size), swap(a_high, axis, b, size))
        known.update(fresh)
        late = a ^ b
    for a in single:
        known.update(
            {o ^ a: tuple(swap(v, axis, a, size) for v in have) for o, have in known.items()}
        )
        late = late or a
    return known, [o for o in known if o & late == late and size > 1]


def gather_depth(x, axis, size):
    known = {0: x}
    for b in reversed(bits_of(size)):
        known.update({o ^ b: swap(v, axis, b, size) for o, v in known.items()})
    return known


def first_kernel(left_ref, right_ref, probe_ref, low_ref, high_ref, turned_ref):
    right = right_ref[0, 0]
    image = lax.dot_general(
        left_ref[0, 0], probe_ref[...], (((0,), (0,)), ((), ())),
        preferred_element_type=jnp.float32,
    ).astype(jnp.bfloat16)
    half = low_ref.shape[0]
    low_ref[...] = jnp.dot(
        right[:half], image, preferred_element_type=jnp.float32
    ).astype(jnp.bfloat16)
    high_ref[...] = jnp.dot(
        right[half:], image, preferred_element_type=jnp.float32
    ).astype(jnp.bfloat16)
    turned_ref[...] = right.T


def couple(turned_ref, low_ref, high_ref):
    half = low_ref.shape[0]
    total = jnp.dot(
        turned_ref[:, :half], low_ref[...], preferred_element_type=jnp.float32
    ) + jnp.dot(turned_ref[:, half:], high_ref[...], preferred_element_type=jnp.float32)
    return total.astype(jnp.bfloat16)


def early_kernel(turned_ref, *refs):
    out_ref = refs[-1]
    for n in range(out_ref.shape[0]):
        out_ref[n] = couple(turned_ref, refs[2 * n], refs[2 * n + 1])


def late_kernel(early, late, wanted_ref, turned_ref, early_ref, *refs):
    out_ref, every_ref = refs[-2:]
    for n, o in enumerate(early):
        every_ref[o] = early_ref[n]
    for n, o in enumerate(late):
        every_ref[o] = couple(turned_ref, refs[2 * n], refs[2 * n + 1])
    width = every_ref.shape[2]
    for t in range(out_ref.shape[1] // width):
        out_ref[:, t * width:(t + 1) * width] = every_ref[wanted_ref[t]]


def partial_sketch(panel, left_refs, coupling_refs):
    total = None
    step = 2 if len(left_refs) % 2 == 0 else 1
    for o in range(0, len(left_refs), step):
        left = jnp.concatenate([left_refs[o + i][panel] for i in range(step)], axis=1)
        coupling = jnp.concatenate([coupling_refs[o + i][...] for i in range(step)], axis=0)
        term = jnp.dot(left, coupling, preferred_element_type=jnp.float32)
        total = term if total is None else total + term
    return total


def part_kernel(count, panel, *refs):
    total = partial_sketch(panel, refs[:count], refs[count:2 * count])
    if len(refs) > 2 * count + 1:
        total = total + refs[2 * count][...]
    refs[-1][...] = total


def sketch_kernel(count, panel, *refs):
    sketch_ref, gram_ref = refs[-2:]
    total = partial_sketch(panel, refs[:count], refs[count:2 * count])
    if len(refs) > 2 * count + 2:
        total = total + refs[2 * count][...]
    listed, packed, width = gram_ref.shape
    half = width // 2
    lane = lax.broadcasted_iota(jnp.int32, (half, width), 1)
    row = lax.broadcasted_iota(jnp.int32, (half, width), 0)
    for t in range(listed):
        tile = total[:, t * width:(t + 1) * width]
        sketch_ref[t] = tile
        gram = lax.dot_general(
            tile, tile, (((0,), (0,)), ((), ())), precision=HIGHEST,
            preferred_element_type=jnp.float32,
        )
        lower = gram[half:]
        gram_ref[t, :half] = jnp.where(lane < row, pltpu.roll(lower, half, axis=1), gram[:half])
        diagonal = jnp.sum(jnp.where(lane == row + half, lower, 0.0), axis=0, keepdims=True)
        gram_ref[t, half:] = jnp.broadcast_to(diagonal, (packed - half, width))


def unpacked(packed, half):
    width = packed.shape[1]
    lane = lax.broadcasted_iota(jnp.int32, (half, width), 1)
    row = lax.broadcasted_iota(jnp.int32, (half, width), 0)
    upper = packed[:half]
    moved = pltpu.roll(upper, half, axis=1)
    diagonal = jnp.broadcast_to(packed[half:half + 1], (half, width))
    strict = jnp.concatenate(
        [jnp.where(lane > row, upper, 0.0),
         jnp.where((lane >= half) & (lane < row + half), moved, 0.0)], axis=0)
    center = jnp.concatenate(
        [jnp.where(lane == row, upper, 0.0),
         jnp.where(lane == row + half, diagonal, 0.0)], axis=0)
    return strict + strict.T + center


def eliminate(panel, first, lane, sub):
    cols = [
        jnp.broadcast_to(panel[:, first + j:first + j + 1], panel.shape) for j in range(BLOCK)
    ]
    upper = jnp.zeros_like(panel)
    inverse = jnp.zeros_like(panel)
    pivots = jnp.zeros_like(panel)
    for j in range(BLOCK):
        k = first + j
        pivot = jnp.broadcast_to(cols[j][j:j + 1, :], panel.shape)
        recip = 1.0 / pivot
        root = lax.rsqrt(pivot)
        factor = jnp.where(sub > j, cols[j] * recip, 0.0)
        for c in range(j + 1, BLOCK):
            cols[c] = cols[c] - factor * jnp.broadcast_to(cols[c][j:j + 1, :], panel.shape)
        row = jnp.broadcast_to(panel[j:j + 1, :], panel.shape)
        here = sub == j
        upper = jnp.where(here & (lane >= k), row * root, upper)
        row = jnp.where(lane == k, 1.0, row)
        inverse = jnp.where(here & (lane <= k), row * root, inverse)
        pivots = jnp.where(here, recip, pivots)
        panel = jnp.where((lane == k) & (sub >= j), jnp.where(here, 1.0, 0.0), panel)
        panel = panel - factor * row
    below = jnp.where(lane >= first + BLOCK, panel * pivots, 0.0)
    panel = jnp.where((lane < first + BLOCK) & (lane > first + sub), 0.0, panel)
    return panel, below, upper, inverse


def factor_kernel(scale, own_ref, other_ref, sketch_ref, basis_ref, chol_ref, work_ref, upper_ref, inverse_ref):
    listed, width, _ = work_ref.shape
    for t in range(listed):
        work_ref[t] = unpacked(own_ref[t] + other_ref[t], width // 2)
    lane = lax.broadcasted_iota(jnp.int32, (BLOCK, width), 1)
    sub = lax.broadcasted_iota(jnp.int32, (BLOCK, width), 0)
    for first in range(0, width, BLOCK):
        last = first + BLOCK
        done = [eliminate(work_ref[t, first:last, :], first, lane, sub) for t in range(listed)]
        for t in range(listed):
            rows, below, upper, inverse = done[t]
            upper_ref[t, first:last, :] = upper
            inverse_ref[t, first:last, :] = inverse * scale
            if last < width:
                at = lax.broadcasted_iota(jnp.int32, (width - last, width), 1)
                old = work_ref[t, last:, :]
                old = jnp.where((at >= first) & (at < last), 0.0, old)
                update = lax.dot_general(
                    below, rows, (((0,), (0,)), ((), ())), precision=HIGHEST,
                    preferred_element_type=jnp.float32,
                )
                work_ref[t, last:, :] = old - update[last:, :]
    for t in range(listed):
        chol_ref[t] = upper_ref[t].T * (1.0 / scale)
        basis_ref[t] = lax.dot_general(
            sketch_ref[t], inverse_ref[t], (((1,), (1,)), ((), ())), precision=HIGHEST,
            preferred_element_type=jnp.float32,
        )


def call(kernel, shapes, *args, **more):
    specs = more.pop("in_specs", [VMEM] * len(args))
    single = not isinstance(shapes, tuple)
    return pl.pallas_call(
        kernel, out_shape=shapes, in_specs=specs,
        out_specs=VMEM if single else (VMEM,) * len(shapes), **more,
    )(*args)


def on_device(rows_size, depth_size, left_factors, right_factors, probe_matrix, tile_list):
    _, panels, tile_size, rank_size = left_factors.shape
    listed = tile_list.shape[1]
    width = probe_matrix.shape[1]
    scale = math.sqrt(float(tile_size))
    me = lax.axis_index("rows")
    level = lax.axis_index("depth")
    part = tile_size // depth_size
    half = tile_size // 2
    bf16, f32 = jnp.bfloat16, jnp.float32
    shape = jax.ShapeDtypeStruct

    found, turned, late = [], [], []
    for p in range(panels):
        low, high, right_turned = pl.pallas_call(
            first_kernel,
            grid=(1,),
            in_specs=[
                pl.BlockSpec((1, 1, tile_size, rank_size), lambda i, p=p: (0, p, 0, 0)),
                pl.BlockSpec((1, 1, tile_size, rank_size), lambda i, p=p: (0, p, 0, 0)),
                pl.BlockSpec((tile_size, width), lambda i: (0, 0)),
            ],
            out_specs=(
                pl.BlockSpec((half, width), lambda i: (0, 0)),
                pl.BlockSpec((half, width), lambda i: (0, 0)),
                pl.BlockSpec((rank_size, tile_size), lambda i: (0, 0)),
            ),
            out_shape=(
                shape((half, width), bf16), shape((half, width), bf16),
                shape((rank_size, tile_size), bf16),
            ),
        )(left_factors, right_factors, probe_matrix)
        blocks, last = gather_rows((low, high), "rows", rows_size)
        found.append(blocks)
        late.append(last)
        turned.append(right_turned)

    blocks = left_factors[0].reshape(panels, depth_size, part, rank_size)
    lefts = []
    for o in range(depth_size):
        block = lax.dynamic_index_in_dim(blocks, level ^ o, 1, keepdims=False)
        lefts.append(swap(block, "depth", o, depth_size) if o else block)

    wanted = lax.dynamic_index_in_dim(tile_list, me, 0, keepdims=False) ^ me
    gathered = []
    for p in range(panels):
        last = late[p]
        early = [o for o in found[p] if o not in last]
        first = call(
            early_kernel, shape((len(early), rank_size, width), bf16),
            turned[p], *[h for o in early for h in found[p][o]],
        )
        rest = [h for o in last for h in found[p][o]]
        coupling = call(
            functools.partial(late_kernel, early, last),
            shape((rank_size, listed * width), bf16),
            wanted, turned[p], first, *rest,
            in_specs=[SMEM] + [VMEM] * (2 + len(rest)),
            scratch_shapes=[pltpu.VMEM((rows_size, rank_size, width), bf16)],
        )
        every = gather_depth(coupling, "depth", depth_size)
        gathered.append([every[o] for o in range(depth_size)])

    total = []
    for p in range(panels - 1):
        total = [call(
            functools.partial(part_kernel, depth_size, p),
            shape((part, listed * width), f32), *lefts, *gathered[p], *total,
        )]
    packed = width // 2 + 8
    sketch, gram = call(
        functools.partial(sketch_kernel, depth_size, panels - 1),
        (shape((listed, part, width), f32), shape((listed, packed, width), f32)),
        *lefts, *gathered[-1], *total,
    )
    other = jnp.zeros_like(gram)
    for b in bits_of(depth_size):
        gram = gram + other
        other = swap(gram, "depth", b, depth_size)
    basis, chol_factor = call(
        functools.partial(factor_kernel, scale),
        (shape((listed, part, width), f32), shape((listed, width, width), f32)),
        gram, other, sketch,
        scratch_shapes=[pltpu.VMEM((listed, width, width), f32)] * 3,
    )
    return (basis[None], chol_factor[None])


def solution(mesh):
    in_specs = (P("rows", "depth", None, None), P("rows", "depth", None, None), P(), P())
    out_specs = (P("rows", None, "depth", None), P("rows", None, None, None))
    body = functools.partial(on_device, mesh.shape["rows"], mesh.shape["depth"])
    return jax.shard_map(body, mesh=mesh, in_specs=in_specs, out_specs=out_specs, check_vma=False)
```

```python
import functools
import math

import jax
import jax.numpy as jnp
from jax import lax
from jax.experimental import pallas as pl
from jax.experimental.pallas import tpu as pltpu
from jax.sharding import PartitionSpec as P


HIGHEST = lax.Precision.HIGHEST
BLOCK = 16
GRANT = 12 << 20
VMEM = pl.BlockSpec(memory_space=pltpu.VMEM)
ANY = pl.BlockSpec(memory_space=pl.ANY)
SMEM = pl.BlockSpec(memory_space=pltpu.SMEM)


def swap(x, axis, bits, size):
    return lax.ppermute(x, axis, [(i, i ^ bits) for i in range(size)])


def bits_of(size):
    return [1 << b for b in range(size.bit_length() - 1)]


def gather_rows(halves, axis, size):
    known = {0: halves}
    bits = bits_of(size)
    pairs = bits[len(bits) % 2:]
    late = 0
    for a, b in zip(pairs[::2], pairs[1::2]):
        fresh = {}
        for o, (low, high) in known.items():
            a_low, a_high = swap(low, axis, a, size), swap(high, axis, a, size)
            b_low, b_high = swap(low, axis, b, size), swap(high, axis, b, size)
            fresh[o ^ a] = (a_low, a_high)
            fresh[o ^ b] = (b_low, b_high)
            fresh[o ^ a ^ b] = (swap(b_low, axis, a, size), swap(a_high, axis, b, size))
        known.update(fresh)
        late = a ^ b
    return known, [o for o in known if late and o & late == late]


def gather_depth(x, axis, size):
    known = {0: x}
    for b in reversed(bits_of(size)):
        fresh = {}
        for o, v in known.items():
            fresh[o ^ b] = swap(v, axis, b, size)
        known.update(fresh)
    return known


def fetch(pairs, sems):
    copies = [pltpu.make_async_copy(src, dst, sems.at[n]) for n, (src, dst) in enumerate(pairs)]
    for copy in copies:
        copy.start()
    return copies


def first_kernel(panels, left_ref, right_ref, probe_ref, *refs):
    outs, (probe_buf, left_buf, right_buf, sems) = refs[:2 * panels], refs[2 * panels:]
    sources = [(probe_ref, probe_buf)]
    for p in range(panels):
        sources += [(left_ref.at[0, p], left_buf.at[p]), (right_ref.at[0, p], right_buf.at[p])]
    copies = fetch(sources, sems)
    copies[0].wait()
    probe_turned = probe_buf[...].T
    for p in range(panels):
        copies[1 + 2 * p].wait()
        image = jnp.dot(
            probe_turned, left_buf[p], preferred_element_type=jnp.float32
        ).astype(jnp.bfloat16)
        copies[2 + 2 * p].wait()
        half = outs[0].shape[0]
        for h in range(2):
            outs[2 * p + h][...] = lax.dot_general(
                right_buf[p, h * half:(h + 1) * half], image, (((1,), (1,)), ((), ())),
                preferred_element_type=jnp.float32,
            ).astype(jnp.bfloat16)


def turn_kernel(right_ref, turned_ref):
    for p in range(turned_ref.shape[0]):
        turned_ref[p] = right_ref[0, p].T


def couple(turned_refs, panel, blocks):
    half = blocks[0][0].shape[0]
    total = None
    for h in range(2):
        left = [ref[panel, :, h * half:(h + 1) * half] for ref in turned_refs]
        left = jnp.concatenate(left, axis=0) if len(left) > 1 else left[0]
        right = [block[h][...] for block in blocks]
        right = jnp.concatenate(right, axis=1) if len(right) > 1 else right[0]
        term = jnp.dot(left, right, preferred_element_type=jnp.float32)
        total = term if total is None else total + term
    return total.astype(jnp.bfloat16)


def early_kernel(panel, sides, count, *refs):
    turned_refs, block_refs, outs = refs[:sides], refs[sides:-sides], refs[-sides:]
    rank, width = outs[0].shape[1:]
    for first in range(0, count, 2):
        blocks = range(first, min(first + 2, count))
        found = couple(turned_refs, panel, [block_refs[2 * n:2 * n + 2] for n in blocks])
        for i, n in enumerate(blocks):
            for s in range(sides):
                outs[s][n] = found[s * rank:(s + 1) * rank, i * width:(i + 1) * width]


def late_kernel(panel, early, late, wanted_ref, turned_ref, *refs):
    sides, count = len(early), len(late)
    early_refs, block_refs = refs[:sides], refs[sides:sides + 2 * count]
    out_ref, every_ref = refs[sides + 2 * count:]
    for s, offsets in enumerate(early):
        for n, o in enumerate(offsets):
            every_ref[o] = early_refs[s][n]
    width = every_ref.shape[2]
    for first in range(0, count, 2):
        blocks = range(first, min(first + 2, count))
        found = couple([turned_ref], panel, [block_refs[2 * n:2 * n + 2] for n in blocks])
        for i, n in enumerate(blocks):
            every_ref[late[n]] = found[:, i * width:(i + 1) * width]
    for t in range(out_ref.shape[1] // width):
        out_ref[:, t * width:(t + 1) * width] = every_ref[wanted_ref[t]]


def partial_sketch(panel, left_refs, coupling_refs):
    total = None
    step = 2 if len(left_refs) % 2 == 0 else 1
    for o in range(0, len(left_refs), step):
        left = jnp.concatenate([left_refs[o + i][panel] for i in range(step)], axis=1)
        coupling = jnp.concatenate([coupling_refs[o + i][...] for i in range(step)], axis=0)
        term = jnp.dot(left, coupling, preferred_element_type=jnp.float32)
        total = term if total is None else total + term
    return total


def part_kernel(count, panel, *refs):
    total = partial_sketch(panel, refs[:count], refs[count:2 * count])
    if len(refs) > 2 * count + 1:
        total = total + refs[2 * count][...]
    refs[-1][...] = total


def sketch_kernel(count, panel, *refs):
    sketch_ref, gram_ref = refs[-2:]
    total = partial_sketch(panel, refs[:count], refs[count:2 * count])
    if len(refs) > 2 * count + 2:
        total = total + refs[2 * count][...]
    listed, packed, width = gram_ref.shape
    half = width // 2
    lane = lax.broadcasted_iota(jnp.int32, (half, width), 1)
    row = lax.broadcasted_iota(jnp.int32, (half, width), 0)
    for t in range(listed):
        tile = total[:, t * width:(t + 1) * width]
        sketch_ref[t] = tile
        gram = lax.dot_general(
            tile, tile, (((0,), (0,)), ((), ())), precision=HIGHEST,
            preferred_element_type=jnp.float32,
        )
        lower = gram[half:]
        gram_ref[t, :half] = jnp.where(lane < row, pltpu.roll(lower, half, axis=1), gram[:half])
        diagonal = jnp.sum(jnp.where(lane == row + half, lower, 0.0), axis=0, keepdims=True)
        gram_ref[t, half:] = jnp.broadcast_to(diagonal, (packed - half, width))


def unpacked(packed, half):
    width = packed.shape[1]
    lane = lax.broadcasted_iota(jnp.int32, (half, width), 1)
    row = lax.broadcasted_iota(jnp.int32, (half, width), 0)
    upper = packed[:half]
    moved = pltpu.roll(upper, half, axis=1)
    diagonal = jnp.broadcast_to(packed[half:half + 1], (half, width))
    strict = jnp.concatenate(
        [jnp.where(lane > row, upper, 0.0),
         jnp.where((lane >= half) & (lane < row + half), moved, 0.0)], axis=0)
    center = jnp.concatenate(
        [jnp.where(lane == row, upper, 0.0),
         jnp.where(lane == row + half, diagonal, 0.0)], axis=0)
    return strict + strict.T + center


def eliminate(panel, first, lane, sub):
    cols = [
        jnp.broadcast_to(panel[:, first + j:first + j + 1], panel.shape) for j in range(BLOCK)
    ]
    upper = jnp.zeros_like(panel)
    inverse = jnp.zeros_like(panel)
    pivots = jnp.zeros_like(panel)
    for j in range(BLOCK):
        k = first + j
        pivot = jnp.broadcast_to(cols[j][j:j + 1, :], panel.shape)
        recip = 1.0 / pivot
        root = lax.rsqrt(pivot)
        factor = jnp.where(sub > j, cols[j] * recip, 0.0)
        for c in range(j + 1, BLOCK):
            cols[c] = cols[c] - factor * jnp.broadcast_to(cols[c][j:j + 1, :], panel.shape)
        row = jnp.broadcast_to(panel[j:j + 1, :], panel.shape)
        here = sub == j
        upper = jnp.where(here & (lane >= k), row * root, upper)
        row = jnp.where(lane == k, 1.0, row)
        inverse = jnp.where(here & (lane <= k), row * root, inverse)
        pivots = jnp.where(here, recip, pivots)
        panel = jnp.where((lane == k) & (sub >= j), jnp.where(here, 1.0, 0.0), panel)
        panel = panel - factor * row
    below = jnp.where(lane >= first + BLOCK, panel * pivots, 0.0)
    panel = jnp.where((lane < first + BLOCK) & (lane > first + sub), 0.0, panel)
    return panel, below, upper, inverse


def factor_kernel(scale, own_ref, other_ref, sketch_ref, basis_ref, chol_ref, work_ref, upper_ref, inverse_ref):
    listed, width, _ = work_ref.shape
    for t in range(listed):
        work_ref[t] = unpacked(own_ref[t] + other_ref[t], width // 2)
    lane = lax.broadcasted_iota(jnp.int32, (BLOCK, width), 1)
    sub = lax.broadcasted_iota(jnp.int32, (BLOCK, width), 0)
    for first in range(0, width, BLOCK):
        last = first + BLOCK
        done = [eliminate(work_ref[t, first:last, :], first, lane, sub) for t in range(listed)]
        for t in range(listed):
            rows, below, upper, inverse = done[t]
            upper_ref[t, first:last, :] = upper
            inverse_ref[t, first:last, :] = inverse * scale
            if last < width:
                at = lax.broadcasted_iota(jnp.int32, (width - last, width), 1)
                old = work_ref[t, last:, :]
                old = jnp.where((at >= first) & (at < last), 0.0, old)
                update = lax.dot_general(
                    below, rows, (((0,), (0,)), ((), ())), precision=HIGHEST,
                    preferred_element_type=jnp.float32,
                )
                work_ref[t, last:, :] = old - update[last:, :]
    for t in range(listed):
        chol_ref[t] = upper_ref[t].T * (1.0 / scale)
        basis_ref[t] = lax.dot_general(
            sketch_ref[t], inverse_ref[t], (((1,), (1,)), ((), ())), precision=HIGHEST,
            preferred_element_type=jnp.float32,
        )


def call(kernel, shapes, *args, in_specs=None, leave=False, **more):
    specs = in_specs or [VMEM] * len(args)
    args = [
        pltpu.with_memory_space_constraint(x, pltpu.VMEM) if spec is VMEM else x
        for x, spec in zip(args, specs)
    ]
    if not leave:
        shapes = jax.tree.map(lambda s: pltpu.VMEM(s.shape, s.dtype), shapes)
    out = VMEM if not isinstance(shapes, tuple) else (VMEM,) * len(shapes)
    params = pltpu.CompilerParams(vmem_limit_bytes=GRANT)
    return pl.pallas_call(
        kernel, out_shape=shapes, in_specs=specs, out_specs=out, compiler_params=params, **more
    )(*args)


def on_device(rows_size, depth_size, left_factors, right_factors, probe_matrix, tile_list):
    _, panels, tile_size, rank_size = left_factors.shape
    listed = tile_list.shape[1]
    width = probe_matrix.shape[1]
    scale = math.sqrt(float(tile_size))
    me = lax.axis_index("rows")
    level = lax.axis_index("depth")
    part = tile_size // depth_size
    half = tile_size // 2
    bf16, f32 = jnp.bfloat16, jnp.float32
    shape = jax.ShapeDtypeStruct

    single = len(bits_of(rows_size)) % 2
    halves = call(
        functools.partial(first_kernel, panels), (shape((half, width), bf16),) * (2 * panels),
        left_factors, right_factors, probe_matrix, in_specs=[ANY] * 3,
        scratch_shapes=[
            pltpu.VMEM((tile_size, width), bf16),
            pltpu.VMEM((panels, tile_size, rank_size), bf16),
            pltpu.VMEM((panels, tile_size, rank_size), bf16),
            pltpu.SemaphoreType.DMA((1 + 2 * panels,)),
        ],
    )
    turned = [call(
        turn_kernel, shape((panels, rank_size, tile_size), bf16), right_factors,
        in_specs=[pl.BlockSpec(right_factors.shape)],
    )]
    if single:
        turned.append(swap(turned[0], "rows", 1, rows_size))
    found, late = [], []
    for p in range(panels):
        blocks, last = gather_rows(halves[2 * p:2 * p + 2], "rows", rows_size)
        found.append(blocks)
        late.append(last)

    blocks = left_factors[0].reshape(panels, depth_size, part, rank_size)
    lefts = []
    for o in range(depth_size):
        block = lax.dynamic_index_in_dim(blocks, level ^ o, 1, keepdims=False)
        lefts.append(swap(block, "depth", o, depth_size) if o else block)

    wanted = lax.dynamic_index_in_dim(tile_list, me, 0, keepdims=False) ^ me
    gathered = []
    for p in range(panels):
        last = late[p]
        early = [o for o in found[p] if o not in last]
        sides = 1 + single
        args = [h for o in early for h in found[p][o]]
        first = call(
            functools.partial(early_kernel, p, sides, len(early)),
            (shape((len(early), rank_size, width), bf16),) * sides,
            *turned, *args,
        )
        coupled, offsets = [first[0]], [early]
        if single:
            coupled.append(swap(first[1], "rows", 1, rows_size))
            offsets.append([o ^ 1 for o in early])
        rest = [h for o in last for h in found[p][o]]
        if single:
            rest += [swap(h, "rows", 1, rows_size) for h in rest]
            last = last + [o ^ 1 for o in last]
        coupling = call(
            functools.partial(late_kernel, p, offsets, last),
            shape((rank_size, listed * width), bf16),
            wanted, turned[0], *coupled, *rest,
            in_specs=[SMEM] + [VMEM] * (1 + len(coupled) + len(rest)),
            scratch_shapes=[pltpu.VMEM((rows_size, rank_size, width), bf16)],
        )
        every = gather_depth(coupling, "depth", depth_size)
        gathered.append([every[o] for o in range(depth_size)])

    total = []
    for p in range(panels - 1):
        total = [call(
            functools.partial(part_kernel, depth_size, p),
            shape((part, listed * width), f32), *lefts, *gathered[p], *total,
        )]
    packed = width // 2 + 8
    sketch, gram = call(
        functools.partial(sketch_kernel, depth_size, panels - 1),
        (shape((listed, part, width), f32), shape((listed, packed, width), f32)),
        *lefts, *gathered[-1], *total,
    )
    other = jnp.zeros_like(gram)
    for b in bits_of(depth_size):
        gram = gram + other
        other = swap(gram, "depth", b, depth_size)
    basis, chol_factor = call(
        functools.partial(factor_kernel, scale),
        (shape((listed, part, width), f32), shape((listed, width, width), f32)),
        gram, other, sketch, leave=True,
        scratch_shapes=[pltpu.VMEM((listed, width, width), f32)] * 3,
    )
    return (basis[None], chol_factor[None])


def solution(mesh):
    in_specs = (P("rows", "depth", None, None), P("rows", "depth", None, None), P(), P())
    out_specs = (P("rows", None, "depth", None), P("rows", None, None, None))

    def body(*args):
        return on_device(mesh.shape["rows"], mesh.shape["depth"], *args)

    return jax.shard_map(body, mesh=mesh, in_specs=in_specs, out_specs=out_specs, check_vma=False)
```

```python
import functools
import math

import jax
import jax.numpy as jnp
from jax import lax
from jax.experimental import pallas as pl
from jax.experimental.pallas import tpu as pltpu
from jax.sharding import PartitionSpec as P


HIGHEST = lax.Precision.HIGHEST
BLOCK = 16
GRANT = 12 << 20
VMEM = pl.BlockSpec(memory_space=pltpu.VMEM)
HBM = pl.BlockSpec(memory_space=pltpu.HBM)
SMEM = pl.BlockSpec(memory_space=pltpu.SMEM)


def swap(x, axis, bits, size):
    return lax.ppermute(x, axis, [(i, i ^ bits) for i in range(size)])


def bits_of(size):
    return [1 << b for b in range(size.bit_length() - 1)]


def gather_rows(halves, axis, size):
    known = {0: halves}
    bits = bits_of(size)
    pairs = bits[len(bits) % 2:]
    late = 0
    for a, b in zip(pairs[::2], pairs[1::2]):
        fresh = {}
        for o, (low, high) in known.items():
            a_high, b_low = swap(high, axis, a, size), swap(low, axis, b, size)
            a_low, b_high = swap(low, axis, a, size), swap(high, axis, b, size)
            fresh[o ^ a] = (a_low, a_high)
            fresh[o ^ b] = (b_low, b_high)
            fresh[o ^ a ^ b] = (swap(b_low, axis, a, size), swap(a_high, axis, b, size))
        known.update(fresh)
        late = a ^ b
    return known, [o for o in known if late and o & late == late]


def gather_depth(x, axis, size):
    known = {0: x}
    for b in reversed(bits_of(size)):
        fresh = {}
        for o, v in known.items():
            fresh[o ^ b] = swap(v, axis, b, size)
        known.update(fresh)
    return known


def fetch(pairs, sems):
    copies = [pltpu.make_async_copy(src, dst, sems.at[n]) for n, (src, dst) in enumerate(pairs)]
    for copy in copies:
        copy.start()
    return copies


def rows_of(probe_turned, left, right, low_ref, high_ref):
    image = jnp.dot(probe_turned, left[...], preferred_element_type=jnp.float32)
    image = image.astype(jnp.bfloat16)
    half = low_ref.shape[0]
    for h, ref in enumerate((low_ref, high_ref)):
        ref[...] = lax.dot_general(
            right[h * half:(h + 1) * half], image, (((1,), (1,)), ((), ())),
            preferred_element_type=jnp.float32,
        ).astype(jnp.bfloat16)


def first_kernel(left_ref, right_ref, probe_ref, low_ref, high_ref, probe_buf, left_buf, right_buf, sems):
    copies = fetch(
        [(probe_ref, probe_buf), (left_ref.at[0, 0], left_buf), (right_ref.at[0, 0], right_buf)], sems
    )
    for copy in copies:
        copy.wait()
    rows_of(probe_buf[...].T, left_buf, right_buf, low_ref, high_ref)


def second_kernel(count, level_ref, left_ref, right_ref, probe_ref, *outs):
    panels = left_ref.shape[1]
    turned_ref, block_refs = outs[2 * panels - 2], outs[2 * panels - 1:]
    probe_turned = probe_ref[...].T
    for p in range(1, panels):
        rows_of(probe_turned, left_ref.at[0, p], right_ref.at[0, p], *outs[2 * p - 2:2 * p])
    part = left_ref.shape[2] // count
    for p in range(panels):
        turned_ref[p] = right_ref[0, p].T
        for o, ref in enumerate(block_refs):
            ref[p] = left_ref[0, p, pl.ds(pl.multiple_of((level_ref[0] ^ o) * part, part), part), :]


def couple(turned_refs, panel, blocks):
    half = blocks[0][0].shape[0]
    total = None
    for h in range(2):
        left = [ref[panel, :, h * half:(h + 1) * half] for ref in turned_refs]
        left = jnp.concatenate(left, axis=0) if len(left) > 1 else left[0]
        right = [block[h][...] for block in blocks]
        right = jnp.concatenate(right, axis=1) if len(right) > 1 else right[0]
        term = jnp.dot(left, right, preferred_element_type=jnp.float32)
        total = term if total is None else total + term
    return total.astype(jnp.bfloat16)


def early_kernel(panel, sides, count, *refs):
    turned_refs, block_refs, outs = refs[:sides], refs[sides:-sides], refs[-sides:]
    rank, width = outs[0].shape[1:]
    for first in range(0, count, 2):
        blocks = range(first, min(first + 2, count))
        found = couple(turned_refs, panel, [block_refs[2 * n:2 * n + 2] for n in blocks])
        for i, n in enumerate(blocks):
            for s in range(sides):
                outs[s][n] = found[s * rank:(s + 1) * rank, i * width:(i + 1) * width]


def late_kernel(panel, early, late, wanted_ref, turned_ref, *refs):
    sides, count = len(early), len(late)
    early_refs, block_refs = refs[:sides], refs[sides:sides + 2 * count]
    out_ref, every_ref = refs[sides + 2 * count:]
    for s, offsets in enumerate(early):
        for n, o in enumerate(offsets):
            every_ref[o] = early_refs[s][n]
    width = every_ref.shape[2]
    for first in range(0, count, 2):
        blocks = range(first, min(first + 2, count))
        found = couple([turned_ref], panel, [block_refs[2 * n:2 * n + 2] for n in blocks])
        for i, n in enumerate(blocks):
            every_ref[late[n]] = found[:, i * width:(i + 1) * width]
    for t in range(out_ref.shape[1] // width):
        out_ref[:, t * width:(t + 1) * width] = every_ref[wanted_ref[t]]


def partial_sketch(panel, left_refs, coupling_refs):
    total = None
    step = 2 if len(left_refs) % 2 == 0 else 1
    for o in range(0, len(left_refs), step):
        left = jnp.concatenate([left_refs[o + i][panel] for i in range(step)], axis=1)
        coupling = jnp.concatenate([coupling_refs[o + i][...] for i in range(step)], axis=0)
        term = jnp.dot(left, coupling, preferred_element_type=jnp.float32)
        total = term if total is None else total + term
    return total


def part_kernel(count, panel, *refs):
    total = partial_sketch(panel, refs[:count], refs[count:2 * count])
    if len(refs) > 2 * count + 1:
        total = total + refs[2 * count][...]
    refs[-1][...] = total


def sketch_kernel(count, panel, *refs):
    sketch_ref, gram_ref = refs[-2:]
    total = partial_sketch(panel, refs[:count], refs[count:2 * count])
    if len(refs) > 2 * count + 2:
        total = total + refs[2 * count][...]
    listed, packed, width = gram_ref.shape
    half = width // 2
    lane = lax.broadcasted_iota(jnp.int32, (half, width), 1)
    row = lax.broadcasted_iota(jnp.int32, (half, width), 0)
    for t in range(listed):
        tile = total[:, t * width:(t + 1) * width]
        sketch_ref[t] = tile
        gram = lax.dot_general(
            tile, tile, (((0,), (0,)), ((), ())), precision=HIGHEST,
            preferred_element_type=jnp.float32,
        )
        lower = gram[half:]
        gram_ref[t, :half] = jnp.where(lane < row, pltpu.roll(lower, half, axis=1), gram[:half])
        diagonal = jnp.sum(jnp.where(lane == row + half, lower, 0.0), axis=0, keepdims=True)
        gram_ref[t, half:] = jnp.broadcast_to(diagonal, (packed - half, width))


def unpacked(packed, half):
    width = packed.shape[1]
    lane = lax.broadcasted_iota(jnp.int32, (half, width), 1)
    row = lax.broadcasted_iota(jnp.int32, (half, width), 0)
    upper = packed[:half]
    moved = pltpu.roll(upper, half, axis=1)
    diagonal = jnp.broadcast_to(packed[half:half + 1], (half, width))
    strict = jnp.concatenate(
        [jnp.where(lane > row, upper, 0.0),
         jnp.where((lane >= half) & (lane < row + half), moved, 0.0)], axis=0)
    center = jnp.concatenate(
        [jnp.where(lane == row, upper, 0.0),
         jnp.where(lane == row + half, diagonal, 0.0)], axis=0)
    return strict + strict.T + center


def eliminate(panel, first, lane, sub):
    cols = [
        jnp.broadcast_to(panel[:, first + j:first + j + 1], panel.shape) for j in range(BLOCK)
    ]
    pivots = jnp.zeros_like(panel)
    recips = jnp.zeros_like(panel)
    for j in range(BLOCK):
        k = first + j
        pivot = jnp.broadcast_to(cols[j][j:j + 1, :], panel.shape)
        recip = 1.0 / pivot
        factor = jnp.where(sub > j, cols[j] * recip, 0.0)
        for c in range(j + 1, BLOCK):
            cols[c] = cols[c] - factor * jnp.broadcast_to(cols[c][j:j + 1, :], panel.shape)
        here = sub == j
        pivots = jnp.where(here, pivot, pivots)
        recips = jnp.where(here, recip, recips)
        row = jnp.where(lane == k, 1.0, jnp.broadcast_to(panel[j:j + 1, :], panel.shape))
        panel = jnp.where((lane == k) & (sub >= j), jnp.where(here, 1.0, 0.0), panel)
        panel = panel - factor * row
    return panel, pivots, recips


def split(x):
    high = x.astype(jnp.bfloat16)
    rest = x - high.astype(jnp.float32)
    mid = rest.astype(jnp.bfloat16)
    return high, mid, (rest - mid.astype(jnp.float32)).astype(jnp.bfloat16)


def outer(a, b):
    (ah, am, al), (bh, bm, bl) = split(a), split(b)
    return lax.dot_general(
        jnp.concatenate([al, ah, am, ah, am, ah], axis=0),
        jnp.concatenate([bh, bl, bm, bm, bh, bh], axis=0),
        (((0,), (0,)), ((), ())), preferred_element_type=jnp.float32,
    )


def factor_kernel(scale, own_ref, other_ref, sketch_ref, basis_ref, chol_ref, work_ref, upper_ref, inverse_ref):
    listed, width, _ = work_ref.shape
    for t in range(listed):
        work_ref[t] = unpacked(own_ref[t] + other_ref[t], width // 2)
    lane = lax.broadcasted_iota(jnp.int32, (BLOCK, width), 1)
    sub = lax.broadcasted_iota(jnp.int32, (BLOCK, width), 0)
    for first in range(0, width, BLOCK):
        last = first + BLOCK
        done = [eliminate(work_ref[t, first:last, :], first, lane, sub) for t in range(listed)]
        for t in range(listed):
            panel, pivots, recips = done[t]
            root = lax.rsqrt(pivots)
            diagonal = lane == first + sub
            upper_ref[t, first:last, :] = jnp.where(
                lane > first + sub, panel * root, jnp.where(diagonal, pivots * root, 0.0)
            )
            inverse_ref[t, first:last, :] = jnp.where(
                lane <= first + sub, panel * (root * scale), 0.0
            )
            if last < width:
                at = lax.broadcasted_iota(jnp.int32, (width - last, width), 1)
                old = work_ref[t, last:, :]
                old = jnp.where((at >= first) & (at < last), 0.0, old)
                below = jnp.where(lane >= last, panel * recips, 0.0)
                rows = jnp.where((lane < last) & (lane > first + sub), 0.0, panel)
                work_ref[t, last:, :] = old - outer(below, rows)[last:, :]
    for t in range(listed):
        chol_ref[t] = upper_ref[t].T * (1.0 / scale)
        basis_ref[t] = lax.dot_general(
            sketch_ref[t], inverse_ref[t], (((1,), (1,)), ((), ())), precision=HIGHEST,
            preferred_element_type=jnp.float32,
        )


def call(kernel, shapes, *args, in_specs=None, leave=False, **more):
    specs = in_specs or [VMEM] * len(args)
    args = [
        x if spec is SMEM else pltpu.with_memory_space_constraint(x, spec.memory_space)
        for x, spec in zip(args, specs)
    ]
    if not leave:
        shapes = jax.tree.map(lambda s: pltpu.VMEM(s.shape, s.dtype), shapes)
    out = VMEM if not isinstance(shapes, tuple) else (VMEM,) * len(shapes)
    params = pltpu.CompilerParams(vmem_limit_bytes=GRANT)
    return pl.pallas_call(
        kernel, out_shape=shapes, in_specs=specs, out_specs=out, compiler_params=params, **more
    )(*args)


def on_device(rows_size, depth_size, left_factors, right_factors, probe_matrix, tile_list):
    _, panels, tile_size, rank_size = left_factors.shape
    listed = tile_list.shape[1]
    width = probe_matrix.shape[1]
    scale = math.sqrt(float(tile_size))
    me = lax.axis_index("rows")
    level = lax.axis_index("depth")
    part = tile_size // depth_size
    half = tile_size // 2
    bf16, f32 = jnp.bfloat16, jnp.float32
    shape = jax.ShapeDtypeStruct

    single = len(bits_of(rows_size)) % 2
    halves = call(
        first_kernel, (shape((half, width), bf16),) * 2,
        left_factors, right_factors, probe_matrix, in_specs=[HBM] * 3,
        scratch_shapes=[
            pltpu.VMEM((tile_size, width), bf16),
            pltpu.VMEM((tile_size, rank_size), bf16),
            pltpu.VMEM((tile_size, rank_size), bf16),
            pltpu.SemaphoreType.DMA((3,)),
        ],
    )
    second = call(
        functools.partial(second_kernel, depth_size),
        (shape((half, width), bf16),) * (2 * panels - 2)
        + (shape((panels, rank_size, tile_size), bf16),)
        + (shape((panels, part, rank_size), bf16),) * depth_size,
        level[None], left_factors, right_factors, probe_matrix, in_specs=[SMEM] + [VMEM] * 3,
    )
    halves = list(halves) + list(second[:2 * panels - 2])
    turned, blocks = [second[2 * panels - 2]], second[2 * panels - 1:]
    if single:
        turned.append(swap(turned[0], "rows", 1, rows_size))
    found, late = [], []
    for p in range(panels):
        reached, last = gather_rows(halves[2 * p:2 * p + 2], "rows", rows_size)
        found.append(reached)
        late.append(last)

    lefts = [swap(x, "depth", o, depth_size) if o else x for o, x in enumerate(blocks)]

    wanted = lax.dynamic_index_in_dim(tile_list, me, 0, keepdims=False) ^ me
    gathered = []
    for p in range(panels):
        last = late[p]
        early = [o for o in found[p] if o not in last]
        sides = 1 + single
        args = [h for o in early for h in found[p][o]]
        first = call(
            functools.partial(early_kernel, p, sides, len(early)),
            (shape((len(early), rank_size, width), bf16),) * sides,
            *turned, *args,
        )
        coupled, offsets = [first[0]], [early]
        if single:
            coupled.append(swap(first[1], "rows", 1, rows_size))
            offsets.append([o ^ 1 for o in early])
        rest = [h for o in last for h in found[p][o]]
        if single:
            rest += [swap(h, "rows", 1, rows_size) for h in rest]
            last = last + [o ^ 1 for o in last]
        coupling = call(
            functools.partial(late_kernel, p, offsets, last),
            shape((rank_size, listed * width), bf16),
            wanted, turned[0], *coupled, *rest,
            in_specs=[SMEM] + [VMEM] * (1 + len(coupled) + len(rest)),
            scratch_shapes=[pltpu.VMEM((rows_size, rank_size, width), bf16)],
        )
        every = gather_depth(coupling, "depth", depth_size)
        gathered.append([every[o] for o in range(depth_size)])

    total = []
    for p in range(panels - 1):
        total = [call(
            functools.partial(part_kernel, depth_size, p),
            shape((part, listed * width), f32), *lefts, *gathered[p], *total,
        )]
    packed = width // 2 + 8
    sketch, gram = call(
        functools.partial(sketch_kernel, depth_size, panels - 1),
        (shape((listed, part, width), f32), shape((listed, packed, width), f32)),
        *lefts, *gathered[-1], *total,
    )
    other = jnp.zeros_like(gram)
    for b in bits_of(depth_size):
        gram = gram + other
        other = swap(gram, "depth", b, depth_size)
    basis, chol_factor = call(
        functools.partial(factor_kernel, scale),
        (shape((listed, part, width), f32), shape((listed, width, width), f32)),
        gram, other, sketch, leave=True,
        scratch_shapes=[pltpu.VMEM((listed, width, width), f32)] * 3,
    )
    return (basis[None], chol_factor[None])


def solution(mesh):
    in_specs = (P("rows", "depth", None, None), P("rows", "depth", None, None), P(), P())
    out_specs = (P("rows", None, "depth", None), P("rows", None, None, None))

    def body(*args):
        return on_device(mesh.shape["rows"], mesh.shape["depth"], *args)

    return jax.shard_map(body, mesh=mesh, in_specs=in_specs, out_specs=out_specs, check_vma=False)
```

```python
import functools
import math

import jax
import jax.numpy as jnp
from jax import lax
from jax.experimental import pallas as pl
from jax.experimental.pallas import tpu as pltpu
from jax.sharding import PartitionSpec as P


HIGHEST = lax.Precision.HIGHEST
BLOCK = 16
GRANT = 12 << 20
VMEM = pl.BlockSpec(memory_space=pltpu.VMEM)
HBM = pl.BlockSpec(memory_space=pltpu.HBM)
SMEM = pl.BlockSpec(memory_space=pltpu.SMEM)


def swap(x, axis, bits, size):
    return lax.ppermute(x, axis, [(i, i ^ bits) for i in range(size)])


def bits_of(size):
    return [1 << b for b in range(size.bit_length() - 1)]


def gather_rows(halves, axis, size):
    known = {0: halves}
    bits = bits_of(size)
    pairs = bits[len(bits) % 2:]
    late = 0
    for a, b in zip(pairs[::2], pairs[1::2]):
        fresh = {}
        for o, (low, high) in known.items():
            a_high, b_low = swap(high, axis, a, size), swap(low, axis, b, size)
            a_low, b_high = swap(low, axis, a, size), swap(high, axis, b, size)
            fresh[o ^ a] = (a_low, a_high)
            fresh[o ^ b] = (b_low, b_high)
            fresh[o ^ a ^ b] = (swap(b_low, axis, a, size), swap(a_high, axis, b, size))
        known.update(fresh)
        late = a ^ b
    return known, [o for o in known if late and o & late == late]


def gather_depth(x, axis, size):
    known = {0: x}
    for b in reversed(bits_of(size)):
        fresh = {}
        for o, v in known.items():
            fresh[o ^ b] = swap(v, axis, b, size)
        known.update(fresh)
    return known


def fetch(pairs, sems):
    copies = [pltpu.make_async_copy(src, dst, sems.at[n]) for n, (src, dst) in enumerate(pairs)]
    for copy in copies:
        copy.start()
    return copies


def rows_of(probe_turned, left, right, low_ref, high_ref):
    image = jnp.dot(probe_turned, left[...], preferred_element_type=jnp.float32)
    image = image.astype(jnp.bfloat16)
    half = low_ref.shape[0]
    for h, ref in enumerate((low_ref, high_ref)):
        ref[...] = lax.dot_general(
            right[h * half:(h + 1) * half], image, (((1,), (1,)), ((), ())),
            preferred_element_type=jnp.float32,
        ).astype(jnp.bfloat16)


def first_kernel(left_ref, right_ref, probe_ref, low_ref, high_ref, probe_buf, left_buf, right_buf, sems):
    copies = fetch(
        [(probe_ref, probe_buf), (left_ref.at[0, 0], left_buf), (right_ref.at[0, 0], right_buf)], sems
    )
    for copy in copies:
        copy.wait()
    rows_of(probe_buf[...].T, left_buf, right_buf, low_ref, high_ref)


def second_kernel(count, level_ref, left_ref, right_ref, probe_ref, *outs):
    panels = left_ref.shape[1]
    outs, (probe_buf, sems) = outs[:-2], outs[-2:]
    turned_ref, block_refs = outs[2 * panels - 2], outs[2 * panels - 1:]
    (copy,) = fetch([(probe_ref, probe_buf)], sems)
    part = left_ref.shape[2] // count
    for p in range(panels):
        turned_ref[p] = right_ref[0, p].T
        for o, ref in enumerate(block_refs):
            ref[p] = left_ref[0, p, pl.ds(pl.multiple_of((level_ref[0] ^ o) * part, part), part), :]
    copy.wait()
    probe_turned = probe_buf[...].T
    for p in range(1, panels):
        rows_of(probe_turned, left_ref.at[0, p], right_ref.at[0, p], *outs[2 * p - 2:2 * p])


def couple(turned_refs, panel, blocks):
    half = blocks[0][0].shape[0]
    total = None
    for h in range(2):
        left = [ref[panel, :, h * half:(h + 1) * half] for ref in turned_refs]
        left = jnp.concatenate(left, axis=0) if len(left) > 1 else left[0]
        right = [block[h][...] for block in blocks]
        right = jnp.concatenate(right, axis=1) if len(right) > 1 else right[0]
        term = jnp.dot(left, right, preferred_element_type=jnp.float32)
        total = term if total is None else total + term
    return total.astype(jnp.bfloat16)


def early_kernel(panel, sides, count, *refs):
    turned_refs, block_refs, outs = refs[:sides], refs[sides:-sides], refs[-sides:]
    rank, width = outs[0].shape[1:]
    for first in range(0, count, 2):
        blocks = range(first, min(first + 2, count))
        found = couple(turned_refs, panel, [block_refs[2 * n:2 * n + 2] for n in blocks])
        for i, n in enumerate(blocks):
            for s in range(sides):
                outs[s][n] = found[s * rank:(s + 1) * rank, i * width:(i + 1) * width]


def late_kernel(panel, early, late, wanted_ref, turned_ref, *refs):
    sides, count = len(early), len(late)
    early_refs, block_refs = refs[:sides], refs[sides:sides + 2 * count]
    out_ref, every_ref = refs[sides + 2 * count:]
    for s, offsets in enumerate(early):
        for n, o in enumerate(offsets):
            every_ref[o] = early_refs[s][n]
    width = every_ref.shape[2]
    for first in range(0, count, 2):
        blocks = range(first, min(first + 2, count))
        found = couple([turned_ref], panel, [block_refs[2 * n:2 * n + 2] for n in blocks])
        for i, n in enumerate(blocks):
            every_ref[late[n]] = found[:, i * width:(i + 1) * width]
    for t in range(out_ref.shape[1] // width):
        out_ref[:, t * width:(t + 1) * width] = every_ref[wanted_ref[t]]


def partial_sketch(panel, left_refs, coupling_refs):
    total = None
    step = 2 if len(left_refs) % 2 == 0 else 1
    for o in range(0, len(left_refs), step):
        left = jnp.concatenate([left_refs[o + i][panel] for i in range(step)], axis=1)
        coupling = jnp.concatenate([coupling_refs[o + i][...] for i in range(step)], axis=0)
        term = jnp.dot(left, coupling, preferred_element_type=jnp.float32)
        total = term if total is None else total + term
    return total


def part_kernel(count, panel, *refs):
    total = partial_sketch(panel, refs[:count], refs[count:2 * count])
    if len(refs) > 2 * count + 1:
        total = total + refs[2 * count][...]
    refs[-1][...] = total


def sketch_kernel(count, panel, *refs):
    sketch_ref, gram_ref = refs[-2:]
    total = partial_sketch(panel, refs[:count], refs[count:2 * count])
    if len(refs) > 2 * count + 2:
        total = total + refs[2 * count][...]
    listed, packed, width = gram_ref.shape
    half = width // 2
    lane = lax.broadcasted_iota(jnp.int32, (half, width), 1)
    row = lax.broadcasted_iota(jnp.int32, (half, width), 0)
    for t in range(listed):
        tile = total[:, t * width:(t + 1) * width]
        sketch_ref[t] = tile
        gram = lax.dot_general(
            tile, tile, (((0,), (0,)), ((), ())), precision=HIGHEST,
            preferred_element_type=jnp.float32,
        )
        lower = gram[half:]
        gram_ref[t, :half] = jnp.where(lane < row, pltpu.roll(lower, half, axis=1), gram[:half])
        diagonal = jnp.sum(jnp.where(lane == row + half, lower, 0.0), axis=0, keepdims=True)
        gram_ref[t, half:] = jnp.broadcast_to(diagonal, (packed - half, width))


def unpacked(packed, half):
    width = packed.shape[1]
    lane = lax.broadcasted_iota(jnp.int32, (half, width), 1)
    row = lax.broadcasted_iota(jnp.int32, (half, width), 0)
    upper = packed[:half]
    moved = pltpu.roll(upper, half, axis=1)
    diagonal = jnp.broadcast_to(packed[half:half + 1], (half, width))
    strict = jnp.concatenate(
        [jnp.where(lane > row, upper, 0.0),
         jnp.where((lane >= half) & (lane < row + half), moved, 0.0)], axis=0)
    center = jnp.concatenate(
        [jnp.where(lane == row, upper, 0.0),
         jnp.where(lane == row + half, diagonal, 0.0)], axis=0)
    return strict + strict.T + center


def eliminate(panel, first, lane, sub):
    cols = [
        jnp.broadcast_to(panel[:, first + j:first + j + 1], panel.shape) for j in range(BLOCK)
    ]
    pivots = jnp.zeros_like(panel)
    recips = jnp.zeros_like(panel)
    for j in range(BLOCK):
        k = first + j
        pivot = jnp.broadcast_to(cols[j][j:j + 1, :], panel.shape)
        recip = 1.0 / pivot
        factor = jnp.where(sub > j, cols[j] * recip, 0.0)
        for c in range(j + 1, BLOCK):
            cols[c] = cols[c] - factor * jnp.broadcast_to(cols[c][j:j + 1, :], panel.shape)
        here = sub == j
        pivots = jnp.where(here, pivot, pivots)
        recips = jnp.where(here, recip, recips)
        row = jnp.where(lane == k, 1.0, jnp.broadcast_to(panel[j:j + 1, :], panel.shape))
        panel = jnp.where((lane == k) & (sub >= j), jnp.where(here, 1.0, 0.0), panel)
        panel = panel - factor * row
    return panel, pivots, recips


def split(x):
    high = x.astype(jnp.bfloat16)
    rest = x - high.astype(jnp.float32)
    mid = rest.astype(jnp.bfloat16)
    return high, mid, (rest - mid.astype(jnp.float32)).astype(jnp.bfloat16)


def outer(a, b):
    (ah, am, al), (bh, bm, bl) = split(a), split(b)
    return lax.dot_general(
        jnp.concatenate([al, ah, am, ah, am, ah], axis=0),
        jnp.concatenate([bh, bl, bm, bm, bh, bh], axis=0),
        (((0,), (0,)), ((), ())), preferred_element_type=jnp.float32,
    )


def factor_kernel(scale, own_ref, other_ref, sketch_ref, basis_ref, chol_ref, work_ref, upper_ref, inverse_ref):
    listed, width, _ = work_ref.shape
    for t in range(listed):
        work_ref[t] = unpacked(own_ref[t] + other_ref[t], width // 2)
    lane = lax.broadcasted_iota(jnp.int32, (BLOCK, width), 1)
    sub = lax.broadcasted_iota(jnp.int32, (BLOCK, width), 0)
    for first in range(0, width, BLOCK):
        last = first + BLOCK
        done = [eliminate(work_ref[t, first:last, :], first, lane, sub) for t in range(listed)]
        for t in range(listed):
            panel, pivots, recips = done[t]
            root = lax.rsqrt(pivots)
            diagonal = lane == first + sub
            upper_ref[t, first:last, :] = jnp.where(
                lane > first + sub, panel * root, jnp.where(diagonal, pivots * root, 0.0)
            )
            inverse_ref[t, first:last, :] = jnp.where(
                lane <= first + sub, panel * (root * scale), 0.0
            )
            if last < width:
                at = lax.broadcasted_iota(jnp.int32, (width - last, width), 1)
                old = work_ref[t, last:, :]
                old = jnp.where((at >= first) & (at < last), 0.0, old)
                below = jnp.where(lane >= last, panel * recips, 0.0)
                rows = jnp.where((lane < last) & (lane > first + sub), 0.0, panel)
                work_ref[t, last:, :] = old - outer(below, rows)[last:, :]
    for t in range(listed):
        chol_ref[t] = upper_ref[t].T * (1.0 / scale)
        basis_ref[t] = lax.dot_general(
            sketch_ref[t], inverse_ref[t], (((1,), (1,)), ((), ())), precision=HIGHEST,
            preferred_element_type=jnp.float32,
        )


def call(kernel, shapes, *args, in_specs=None, leave=False, **more):
    specs = in_specs or [VMEM] * len(args)
    args = [
        x if spec is SMEM else pltpu.with_memory_space_constraint(x, spec.memory_space)
        for x, spec in zip(args, specs)
    ]
    if not leave:
        shapes = jax.tree.map(lambda s: pltpu.VMEM(s.shape, s.dtype), shapes)
    out = VMEM if not isinstance(shapes, tuple) else (VMEM,) * len(shapes)
    params = pltpu.CompilerParams(vmem_limit_bytes=GRANT)
    return pl.pallas_call(
        kernel, out_shape=shapes, in_specs=specs, out_specs=out, compiler_params=params, **more
    )(*args)


def on_device(rows_size, depth_size, left_factors, right_factors, probe_matrix, tile_list):
    _, panels, tile_size, rank_size = left_factors.shape
    listed = tile_list.shape[1]
    width = probe_matrix.shape[1]
    scale = math.sqrt(float(tile_size))
    me = lax.axis_index("rows")
    level = lax.axis_index("depth")
    part = tile_size // depth_size
    half = tile_size // 2
    bf16, f32 = jnp.bfloat16, jnp.float32
    shape = jax.ShapeDtypeStruct

    single = len(bits_of(rows_size)) % 2
    halves = call(
        first_kernel, (shape((half, width), bf16),) * 2,
        left_factors, right_factors, probe_matrix, in_specs=[HBM] * 3,
        scratch_shapes=[
            pltpu.VMEM((tile_size, width), bf16),
            pltpu.VMEM((tile_size, rank_size), bf16),
            pltpu.VMEM((tile_size, rank_size), bf16),
            pltpu.SemaphoreType.DMA((3,)),
        ],
    )
    second = call(
        functools.partial(second_kernel, depth_size),
        (shape((half, width), bf16),) * (2 * panels - 2)
        + (shape((panels, rank_size, tile_size), bf16),)
        + (shape((panels, part, rank_size), bf16),) * depth_size,
        level[None], left_factors, right_factors, probe_matrix,
        in_specs=[SMEM, VMEM, VMEM, HBM],
        scratch_shapes=[pltpu.VMEM((tile_size, width), bf16), pltpu.SemaphoreType.DMA((1,))],
    )
    halves = list(halves) + list(second[:2 * panels - 2])
    turned, blocks = [second[2 * panels - 2]], second[2 * panels - 1:]
    if single:
        turned.append(swap(turned[0], "rows", 1, rows_size))
    found, late = [], []
    for p in range(panels):
        reached, last = gather_rows(halves[2 * p:2 * p + 2], "rows", rows_size)
        found.append(reached)
        late.append(last)

    lefts = [swap(x, "depth", o, depth_size) if o else x for o, x in enumerate(blocks)]

    wanted = lax.dynamic_index_in_dim(tile_list, me, 0, keepdims=False) ^ me
    gathered = []
    for p in range(panels):
        last = late[p]
        early = [o for o in found[p] if o not in last]
        sides = 1 + single
        args = [h for o in early for h in found[p][o]]
        first = call(
            functools.partial(early_kernel, p, sides, len(early)),
            (shape((len(early), rank_size, width), bf16),) * sides,
            *turned, *args,
        )
        coupled, offsets = [first[0]], [early]
        if single:
            coupled.append(swap(first[1], "rows", 1, rows_size))
            offsets.append([o ^ 1 for o in early])
        rest = [h for o in last for h in found[p][o]]
        if single:
            rest += [swap(h, "rows", 1, rows_size) for h in rest]
            last = last + [o ^ 1 for o in last]
        coupling = call(
            functools.partial(late_kernel, p, offsets, last),
            shape((rank_size, listed * width), bf16),
            wanted, turned[0], *coupled, *rest,
            in_specs=[SMEM] + [VMEM] * (1 + len(coupled) + len(rest)),
            scratch_shapes=[pltpu.VMEM((rows_size, rank_size, width), bf16)],
        )
        every = gather_depth(coupling, "depth", depth_size)
        gathered.append([every[o] for o in range(depth_size)])

    total = []
    for p in range(panels - 1):
        total = [call(
            functools.partial(part_kernel, depth_size, p),
            shape((part, listed * width), f32), *lefts, *gathered[p], *total,
        )]
    packed = width // 2 + 8
    sketch, gram = call(
        functools.partial(sketch_kernel, depth_size, panels - 1),
        (shape((listed, part, width), f32), shape((listed, packed, width), f32)),
        *lefts, *gathered[-1], *total,
    )
    other = jnp.zeros_like(gram)
    for b in bits_of(depth_size):
        gram = gram + other
        other = swap(gram, "depth", b, depth_size)
    basis, chol_factor = call(
        functools.partial(factor_kernel, scale),
        (shape((listed, part, width), f32), shape((listed, width, width), f32)),
        gram, other, sketch, leave=True,
        scratch_shapes=[pltpu.VMEM((listed, width, width), f32)] * 3,
    )
    return (basis[None], chol_factor[None])


def solution(mesh):
    in_specs = (P("rows", "depth", None, None), P("rows", "depth", None, None), P(), P())
    out_specs = (P("rows", None, "depth", None), P("rows", None, None, None))

    def body(*args):
        return on_device(mesh.shape["rows"], mesh.shape["depth"], *args)

    return jax.shard_map(body, mesh=mesh, in_specs=in_specs, out_specs=out_specs, check_vma=False)
```

```python
import functools
import math

import jax
import jax.numpy as jnp
from jax import lax
from jax.experimental import pallas as pl
from jax.experimental.pallas import tpu as pltpu
from jax.sharding import PartitionSpec as P


HIGHEST = lax.Precision.HIGHEST
BLOCK = 16
GRANT = 12 << 20
VMEM = pl.BlockSpec(memory_space=pltpu.VMEM)
HBM = pl.BlockSpec(memory_space=pltpu.HBM)
SMEM = pl.BlockSpec(memory_space=pltpu.SMEM)


def swap(x, axis, bits, size):
    return lax.ppermute(x, axis, [(i, i ^ bits) for i in range(size)])


def bits_of(size):
    return [1 << b for b in range(size.bit_length() - 1)]


def gather_rows(halves, axis, size):
    known = {0: halves}
    bits = bits_of(size)
    pairs = bits[len(bits) % 2:]
    late = 0
    for a, b in zip(pairs[::2], pairs[1::2]):
        fresh = {}
        for o, (low, high) in known.items():
            a_high, b_low = swap(high, axis, a, size), swap(low, axis, b, size)
            a_low, b_high = swap(low, axis, a, size), swap(high, axis, b, size)
            fresh[o ^ a] = (a_low, a_high)
            fresh[o ^ b] = (b_low, b_high)
            fresh[o ^ a ^ b] = (swap(b_low, axis, a, size), swap(a_high, axis, b, size))
        known.update(fresh)
        late = a ^ b
    return known, [o for o in known if late and o & late == late]


def gather_depth(x, axis, size):
    known = {0: x}
    for b in reversed(bits_of(size)):
        fresh = {}
        for o, v in known.items():
            fresh[o ^ b] = swap(v, axis, b, size)
        known.update(fresh)
    return known


def fetch(pairs, sems):
    copies = [pltpu.make_async_copy(src, dst, sems.at[n]) for n, (src, dst) in enumerate(pairs)]
    for copy in copies:
        copy.start()
    return copies


def rows_of(probe_turned, left, right, low_ref, high_ref):
    image = jnp.dot(probe_turned, left[...], preferred_element_type=jnp.float32)
    image = image.astype(jnp.bfloat16)
    half = low_ref.shape[0]
    for h, ref in enumerate((low_ref, high_ref)):
        ref[...] = lax.dot_general(
            right[h * half:(h + 1) * half], image, (((1,), (1,)), ((), ())),
            preferred_element_type=jnp.float32,
        ).astype(jnp.bfloat16)


def first_kernel(left_ref, right_ref, probe_ref, low_ref, high_ref, probe_buf, left_buf, right_buf, sems):
    copies = fetch(
        [(probe_ref, probe_buf), (left_ref.at[0, 0], left_buf), (right_ref.at[0, 0], right_buf)], sems
    )
    for copy in copies:
        copy.wait()
    rows_of(probe_buf[...].T, left_buf, right_buf, low_ref, high_ref)


def second_kernel(count, level_ref, left_ref, right_ref, probe_ref, *outs):
    panels = left_ref.shape[1]
    outs, (probe_buf, sems) = outs[:-2], outs[-2:]
    turned_ref, block_refs = outs[2 * panels - 2], outs[2 * panels - 1:]
    (copy,) = fetch([(probe_ref, probe_buf)], sems)
    part = left_ref.shape[2] // count
    for p in range(panels):
        turned_ref[p] = right_ref[0, p].T
        for o, ref in enumerate(block_refs):
            ref[p] = left_ref[0, p, pl.ds(pl.multiple_of((level_ref[0] ^ o) * part, part), part), :]
    copy.wait()
    probe_turned = probe_buf[...].T
    for p in range(1, panels):
        rows_of(probe_turned, left_ref.at[0, p], right_ref.at[0, p], *outs[2 * p - 2:2 * p])


def couple(turned_refs, panel, blocks):
    half = blocks[0][0].shape[0]
    total = None
    for h in range(2):
        left = [ref[panel, :, h * half:(h + 1) * half] for ref in turned_refs]
        left = jnp.concatenate(left, axis=0) if len(left) > 1 else left[0]
        right = [block[h][...] for block in blocks]
        right = jnp.concatenate(right, axis=1) if len(right) > 1 else right[0]
        term = jnp.dot(left, right, preferred_element_type=jnp.float32)
        total = term if total is None else total + term
    return total.astype(jnp.bfloat16)


def early_kernel(panel, sides, count, *refs):
    turned_refs, block_refs, outs = refs[:sides], refs[sides:-sides], refs[-sides:]
    rank, width = outs[0].shape[1:]
    for first in range(0, count, 2):
        blocks = range(first, min(first + 2, count))
        found = couple(turned_refs, panel, [block_refs[2 * n:2 * n + 2] for n in blocks])
        for i, n in enumerate(blocks):
            for s in range(sides):
                outs[s][n] = found[s * rank:(s + 1) * rank, i * width:(i + 1) * width]


def late_kernel(panel, early, late, wanted_ref, turned_ref, *refs):
    sides, count = len(early), len(late)
    early_refs, block_refs = refs[:sides], refs[sides:sides + 2 * count]
    out_ref, every_ref = refs[sides + 2 * count:]
    for s, offsets in enumerate(early):
        for n, o in enumerate(offsets):
            every_ref[o] = early_refs[s][n]
    width = every_ref.shape[2]
    for first in range(0, count, 2):
        blocks = range(first, min(first + 2, count))
        found = couple([turned_ref], panel, [block_refs[2 * n:2 * n + 2] for n in blocks])
        for i, n in enumerate(blocks):
            every_ref[late[n]] = found[:, i * width:(i + 1) * width]
    for t in range(out_ref.shape[1] // width):
        out_ref[:, t * width:(t + 1) * width] = every_ref[wanted_ref[t]]


def partial_sketch(panel, left_refs, coupling_refs):
    total = None
    step = 2 if len(left_refs) % 2 == 0 else 1
    for o in range(0, len(left_refs), step):
        left = jnp.concatenate([left_refs[o + i][panel] for i in range(step)], axis=1)
        coupling = jnp.concatenate([coupling_refs[o + i][...] for i in range(step)], axis=0)
        term = jnp.dot(left, coupling, preferred_element_type=jnp.float32)
        total = term if total is None else total + term
    return total


def part_kernel(count, panel, *refs):
    total = partial_sketch(panel, refs[:count], refs[count:2 * count])
    if len(refs) > 2 * count + 1:
        total = total + refs[2 * count][...]
    refs[-1][...] = total


def sketch_kernel(count, panel, *refs):
    sketch_ref, gram_ref = refs[-2:]
    total = partial_sketch(panel, refs[:count], refs[count:2 * count])
    if len(refs) > 2 * count + 2:
        total = total + refs[2 * count][...]
    listed, packed, width = gram_ref.shape
    half = width // 2
    lane = lax.broadcasted_iota(jnp.int32, (half, width), 1)
    row = lax.broadcasted_iota(jnp.int32, (half, width), 0)
    for t in range(listed):
        tile = total[:, t * width:(t + 1) * width]
        sketch_ref[t] = tile
        gram = lax.dot_general(
            tile, tile, (((0,), (0,)), ((), ())), precision=HIGHEST,
            preferred_element_type=jnp.float32,
        )
        lower = gram[half:]
        gram_ref[t, :half] = jnp.where(lane < row, pltpu.roll(lower, half, axis=1), gram[:half])
        diagonal = jnp.sum(jnp.where(lane == row + half, lower, 0.0), axis=0, keepdims=True)
        gram_ref[t, half:] = jnp.broadcast_to(diagonal, (packed - half, width))


def unpacked(packed, half):
    width = packed.shape[1]
    lane = lax.broadcasted_iota(jnp.int32, (half, width), 1)
    row = lax.broadcasted_iota(jnp.int32, (half, width), 0)
    upper = packed[:half]
    moved = pltpu.roll(upper, half, axis=1)
    diagonal = jnp.broadcast_to(packed[half:half + 1], (half, width))
    strict = jnp.concatenate(
        [jnp.where(lane > row, upper, 0.0),
         jnp.where((lane >= half) & (lane < row + half), moved, 0.0)], axis=0)
    center = jnp.concatenate(
        [jnp.where(lane == row, upper, 0.0),
         jnp.where(lane == row + half, diagonal, 0.0)], axis=0)
    return strict + strict.T + center


def at_row(x, r):
    return jnp.broadcast_to(x[r:r + 1, :], x.shape)


def eliminate(panels, first, lane, sub):
    number = len(panels)
    count, size = panels[0].shape[0] // 8, panels[0].shape[1] // number
    blocks = [[panel[8 * i:8 * i + 8] for i in range(count)] for panel in panels]
    cols = []
    for k in range(first, first + 8 * count):
        col = []
        for i in range(count):
            packed = None
            for t in range(number):
                x = jnp.broadcast_to(blocks[t][i][:, k:k + 1], lane.shape)
                packed = x if packed is None else jnp.where(lane >= t * size, x, packed)
            col.append(packed)
        cols.append(col)
    pivots = [jnp.zeros_like(blocks[0][0])] * count
    recips = [jnp.zeros_like(blocks[0][0])] * count
    factors = []
    for j, col in enumerate(cols):
        s, r = divmod(j, 8)
        pivot = at_row(col[s], r)
        recip = 1.0 / pivot
        factor = {i: col[i] * recip for i in range(s, count)}
        factor[s] = jnp.where(sub > r, factor[s], 0.0)
        for other in cols[j + 1:]:
            top = at_row(other[s], r)
            for i in range(s, count):
                other[i] = other[i] - factor[i] * top
        pivots[s] = jnp.where(sub == r, pivot, pivots[s])
        recips[s] = jnp.where(sub == r, recip, recips[s])
        factors.append(factor)
    done = []
    for t in range(number):
        def own(x):
            return jnp.broadcast_to(x[:, t * size:t * size + 1], x.shape)

        rows = blocks[t]
        for j, factor in enumerate(factors):
            s, r = divmod(j, 8)
            here = lane == first + j
            row = jnp.where(here, 1.0, at_row(rows[s], r))
            for i in range(s, count):
                if i > s:
                    old = jnp.where(here, 0.0, rows[i])
                else:
                    old = jnp.where(here & (sub >= r), jnp.where(sub == r, 1.0, 0.0), rows[i])
                rows[i] = old - own(factor[i]) * row
        done.append([
            jnp.concatenate(parts, axis=0)
            for parts in (rows, [own(x) for x in pivots], [own(x) for x in recips])
        ])
    return done


def split(x):
    high = x.astype(jnp.bfloat16)
    rest = x - high.astype(jnp.float32)
    mid = rest.astype(jnp.bfloat16)
    return high, mid, (rest - mid.astype(jnp.float32)).astype(jnp.bfloat16)


def outer(a, b):
    (ah, am, al), (bh, bm, bl) = split(a), split(b)
    return lax.dot_general(
        jnp.concatenate([al, ah, am, ah, am, ah], axis=0),
        jnp.concatenate([bh, bl, bm, bm, bh, bh], axis=0),
        (((0,), (0,)), ((), ())), preferred_element_type=jnp.float32,
    )


def factor_kernel(scale, own_ref, other_ref, sketch_ref, basis_ref, chol_ref, work_ref, upper_ref, inverse_ref):
    listed, width, _ = work_ref.shape
    for t in range(listed):
        work_ref[t] = unpacked(own_ref[t] + other_ref[t], width // 2)
    lane = lax.broadcasted_iota(jnp.int32, (BLOCK, width), 1)
    sub = lax.broadcasted_iota(jnp.int32, (BLOCK, width), 0)
    for first in range(0, width, BLOCK):
        last = first + BLOCK
        done = eliminate(
            [work_ref[t, first:last, :] for t in range(listed)], first, lane[:8], sub[:8]
        )
        for t in range(listed):
            panel, pivots, recips = done[t]
            root = lax.rsqrt(pivots)
            diagonal = lane == first + sub
            upper_ref[t, first:last, :] = jnp.where(
                lane > first + sub, panel * root, jnp.where(diagonal, pivots * root, 0.0)
            )
            inverse_ref[t, first:last, :] = jnp.where(
                lane <= first + sub, panel * (root * scale), 0.0
            )
            if last < width:
                at = lax.broadcasted_iota(jnp.int32, (width - last, width), 1)
                old = work_ref[t, last:, :]
                old = jnp.where((at >= first) & (at < last), 0.0, old)
                below = jnp.where(lane >= last, panel * recips, 0.0)
                rows = jnp.where((lane < last) & (lane > first + sub), 0.0, panel)
                work_ref[t, last:, :] = old - outer(below, rows)[last:, :]
    for t in range(listed):
        chol_ref[t] = upper_ref[t].T * (1.0 / scale)
        basis_ref[t] = lax.dot_general(
            sketch_ref[t], inverse_ref[t], (((1,), (1,)), ((), ())), precision=HIGHEST,
            preferred_element_type=jnp.float32,
        )


def call(kernel, shapes, *args, in_specs=None, leave=False, **more):
    specs = in_specs or [VMEM] * len(args)
    args = [
        x if spec is SMEM else pltpu.with_memory_space_constraint(x, spec.memory_space)
        for x, spec in zip(args, specs)
    ]
    if not leave:
        shapes = jax.tree.map(lambda s: pltpu.VMEM(s.shape, s.dtype), shapes)
    out = VMEM if not isinstance(shapes, tuple) else (VMEM,) * len(shapes)
    params = pltpu.CompilerParams(vmem_limit_bytes=GRANT)
    return pl.pallas_call(
        kernel, out_shape=shapes, in_specs=specs, out_specs=out, compiler_params=params, **more
    )(*args)


def on_device(rows_size, depth_size, left_factors, right_factors, probe_matrix, tile_list):
    _, panels, tile_size, rank_size = left_factors.shape
    listed = tile_list.shape[1]
    width = probe_matrix.shape[1]
    scale = math.sqrt(float(tile_size))
    me = lax.axis_index("rows")
    level = lax.axis_index("depth")
    part = tile_size // depth_size
    half = tile_size // 2
    bf16, f32 = jnp.bfloat16, jnp.float32
    shape = jax.ShapeDtypeStruct

    single = len(bits_of(rows_size)) % 2
    halves = call(
        first_kernel, (shape((half, width), bf16),) * 2,
        left_factors, right_factors, probe_matrix, in_specs=[HBM] * 3,
        scratch_shapes=[
            pltpu.VMEM((tile_size, width), bf16),
            pltpu.VMEM((tile_size, rank_size), bf16),
            pltpu.VMEM((tile_size, rank_size), bf16),
            pltpu.SemaphoreType.DMA((3,)),
        ],
    )
    *halves, later_left, later_right = lax.optimization_barrier((*halves, left_factors, right_factors))
    second = call(
        functools.partial(second_kernel, depth_size),
        (shape((half, width), bf16),) * (2 * panels - 2)
        + (shape((panels, rank_size, tile_size), bf16),)
        + (shape((panels, part, rank_size), bf16),) * depth_size,
        level[None], later_left, later_right, probe_matrix,
        in_specs=[SMEM, VMEM, VMEM, HBM],
        scratch_shapes=[pltpu.VMEM((tile_size, width), bf16), pltpu.SemaphoreType.DMA((1,))],
    )
    halves = list(halves) + list(second[:2 * panels - 2])
    turned, blocks = [second[2 * panels - 2]], second[2 * panels - 1:]
    if single:
        turned.append(swap(turned[0], "rows", 1, rows_size))
    found, late = [], []
    for p in range(panels):
        reached, last = gather_rows(halves[2 * p:2 * p + 2], "rows", rows_size)
        found.append(reached)
        late.append(last)

    lefts = [swap(x, "depth", o, depth_size) if o else x for o, x in enumerate(blocks)]

    wanted = lax.dynamic_index_in_dim(tile_list, me, 0, keepdims=False) ^ me
    gathered = []
    for p in range(panels):
        last = late[p]
        early = [o for o in found[p] if o not in last]
        sides = 1 + single
        args = [h for o in early for h in found[p][o]]
        first = call(
            functools.partial(early_kernel, p, sides, len(early)),
            (shape((len(early), rank_size, width), bf16),) * sides,
            *turned, *args,
        )
        coupled, offsets = [first[0]], [early]
        if single:
            coupled.append(swap(first[1], "rows", 1, rows_size))
            offsets.append([o ^ 1 for o in early])
        rest = [h for o in last for h in found[p][o]]
        if single:
            rest += [swap(h, "rows", 1, rows_size) for h in rest]
            last = last + [o ^ 1 for o in last]
        coupling = call(
            functools.partial(late_kernel, p, offsets, last),
            shape((rank_size, listed * width), bf16),
            wanted, turned[0], *coupled, *rest,
            in_specs=[SMEM] + [VMEM] * (1 + len(coupled) + len(rest)),
            scratch_shapes=[pltpu.VMEM((rows_size, rank_size, width), bf16)],
        )
        every = gather_depth(coupling, "depth", depth_size)
        gathered.append([every[o] for o in range(depth_size)])

    total = []
    for p in range(panels - 1):
        total = [call(
            functools.partial(part_kernel, depth_size, p),
            shape((part, listed * width), f32), *lefts, *gathered[p], *total,
        )]
    packed = width // 2 + 8
    sketch, gram = call(
        functools.partial(sketch_kernel, depth_size, panels - 1),
        (shape((listed, part, width), f32), shape((listed, packed, width), f32)),
        *lefts, *gathered[-1], *total,
    )
    other = jnp.zeros_like(gram)
    for b in bits_of(depth_size):
        gram = gram + other
        other = swap(gram, "depth", b, depth_size)
    basis, chol_factor = call(
        functools.partial(factor_kernel, scale),
        (shape((listed, part, width), f32), shape((listed, width, width), f32)),
        gram, other, sketch, leave=True,
        scratch_shapes=[pltpu.VMEM((listed, width, width), f32)] * 3,
    )
    return (basis[None], chol_factor[None])


def solution(mesh):
    in_specs = (P("rows", "depth", None, None), P("rows", "depth", None, None), P(), P())
    out_specs = (P("rows", None, "depth", None), P("rows", None, None, None))

    def body(*args):
        return on_device(mesh.shape["rows"], mesh.shape["depth"], *args)

    return jax.shard_map(body, mesh=mesh, in_specs=in_specs, out_specs=out_specs, check_vma=False)
```
